32 devices in a mesh: row: 8 (over y, x, core), col: 4 (over z).
Axes of the slice: x: 2, y: 2, z: 4, core: 2. Of those that a mesh axis runs over, the one named last changes fastest.
Arguments:
- block_values: bfloat16 [8, 4, 64, 256, 256], P('row', 'col'), may hold values from -0.1875 to 0.1875
- block_rows: int32 [8, 4, 64], P('row', 'col'), may hold values from 0 to 63
- block_cols: int32 [8, 4, 64], P('row', 'col'), may hold values from 0 to 255
- live_count: int32 [8, 4], P('row', 'col'), may hold values from 16 to 64, as said below
- objective: float32 [262144], P('col'), may hold values from -6 to 6
- upper_bound: float32 [262144], P('col'), may hold values from 0.5 to 2
- demand: float32 [131072], P('row'), may hold values from -6 to 6
- primal_start: float32 [262144], P('col'), may hold values from 0 to 0.5
- dual_start: float32 [131072], P('row'), may hold values from 0 to 0.5
- restart_at: int32 [8], replicated, may hold values 0 or 1
Outputs:
- primal_final: float32 [262144], P('col')
- dual_final: float32 [131072], P('row')
The draws below stay inside these ranges and needn't reach their ends.
Inputs may be any that keep to these rules, and one draw needn't show every extreme that they name: `live_count`: each device's count of used slots; some device uses all 64.
All inputs are finite; a program needn't handle non-finite values.
Results may differ from the reference program's by a relative error of at most 0.0018.
Values may be sent and summed in bfloat16 or wider, within the bound.
A program may use at most 64 MiB of HBM per device.

```python
import math
import jax
import jax.numpy as jnp
from jax import lax

BS = 256
NB = 64
RB = 64
CB = 256
ITERS = 8
ROWS = 131072
COLS = 262144
N_ROW = 8
N_COL = 4


def draw_live_count(key, part):
    base_counts = jax.random.randint(key, (N_ROW * N_COL,), NB // 4, NB + 1)
    chosen = jax.random.randint(jax.random.fold_in(key, 7), (), 0, N_ROW * N_COL)
    filled = jnp.where(jnp.arange(N_ROW * N_COL) == chosen, NB, base_counts)
    return filled.reshape(N_ROW, N_COL).astype(jnp.int32)


def with_ends(result, rng, low, high):
    longest = result.shape.index(max(result.shape))
    spots = []
    for shift in (0, 1):
        where = [jax.random.randint(jax.random.fold_in(rng, axis), (), 0, length) for axis, length in enumerate(result.shape)]
        where[longest] = (where[longest] + shift) % result.shape[longest]
        spots.append(tuple(where))
    return result.at[spots[0]].set(low).at[spots[1]].set(high)


def levels(stream_key, extent, split, smallest, largest):
    def one(dim, shards_of):
        steps = jax.random.uniform(jax.random.fold_in(jax.random.fold_in(stream_key, 6), dim), (shards_of,), jnp.float32, smallest / len(split), largest / len(split))
        return jnp.repeat(jnp.exp(steps), extent[dim] // shards_of).reshape((-1,) + (1,) * (len(extent) - dim - 1))

    factor_of = one(*split[0])
    for cut in split[1:]:
        factor_of = factor_of * one(*cut)
    return factor_of


def noise(own_key, extent, scale, reach, cuts=(), kind=jnp.bfloat16):
    array = jax.random.normal(own_key, extent, jnp.float32) * scale
    if len(cuts) > 0:
        array = levels(own_key, extent, cuts, -0.22, 0.18) * array
    return jnp.clip(array, min=-reach, max=reach).astype(kind)


def setup_inputs(seed: int = 0) -> dict:
    splits = jax.random.split(jax.random.key(seed), 11)
    return {
        "block_values": noise(splits[0], (N_ROW, N_COL, NB, BS, BS), (4 * BS) ** -0.5, 0.1875, ((0, 8), (1, 4))),
        "block_rows": with_ends(jax.random.randint(splits[1], (N_ROW, N_COL, NB), 0, RB), jax.random.fold_in(splits[1], 1), 0, RB - 1).astype(jnp.int32),
        "block_cols": with_ends(jax.random.randint(splits[2], (N_ROW, N_COL, NB), 0, CB), jax.random.fold_in(splits[2], 1), 0, CB - 1).astype(jnp.int32),
        "live_count": draw_live_count(jax.random.fold_in(splits[10], 71), 0),
        "objective": noise(splits[4], (COLS,), 1.0, 6.0, ((0, 4),), jnp.float32),
        "upper_bound": jnp.clip(jnp.exp(math.log(2.0) - 1.3862944 * jax.random.uniform(splits[5], (COLS,), jnp.float32) ** levels(splits[5], (COLS,), ((0, 4),), -0.2, 0.2)), 0.5, 2.0),
        "demand": noise(splits[6], (ROWS,), 1.0, 6.0, ((0, 8),), jnp.float32),
        "primal_start": jnp.clip(0.5 * jax.random.uniform(splits[7], (COLS,), jnp.float32) ** levels(splits[7], (COLS,), ((0, 4),), -0.2, 0.2), 0.0, 0.5),
        "dual_start": jnp.clip(0.5 * jax.random.uniform(splits[8], (ROWS,), jnp.float32) ** levels(splits[8], (ROWS,), ((0, 8),), -0.2, 0.2), 0.0, 0.5),
        "restart_at": with_ends((jax.random.randint(splits[9], (ITERS,), 0, 2) < 1).astype(jnp.int32), jax.random.fold_in(splits[9], 1), 0, 1),
    }


step_scale = 0.3
epsilon = 1e-06

def dual_part(slot_values, rows_index, cols_index, used_slots, y_group):
    slots = slot_values.shape[0]
    block_size = slot_values.shape[1]
    live_slot = (jnp.arange(slots, dtype=jnp.int32) < used_slots).astype(jnp.float32)
    pieces = y_group.astype(jnp.bfloat16).reshape(-1, block_size)[rows_index].astype(jnp.float32)
    products = jnp.einsum('tij,ti->tj', slot_values.astype(jnp.float32), pieces, precision=lax.Precision.HIGHEST)
    products = products * live_slot[:, None]
    return jax.ops.segment_sum(products, cols_index, num_segments=CB).reshape(-1)

def primal_part(slot_values, rows_index, cols_index, used_slots, x_group):
    slots = slot_values.shape[0]
    block_size = slot_values.shape[1]
    live_slot = (jnp.arange(slots, dtype=jnp.int32) < used_slots).astype(jnp.float32)
    pieces = x_group.reshape(-1, block_size)[cols_index].astype(jnp.float32)
    products = jnp.einsum('tij,tj->ti', slot_values.astype(jnp.float32), pieces, precision=lax.Precision.HIGHEST)
    products = products * live_slot[:, None]
    return jax.ops.segment_sum(products, rows_index, num_segments=RB).reshape(-1)

def reference(block_values, block_rows, block_cols, live_count, objective, upper_bound, demand, primal_start, dual_start, restart_at):

    def dual_total(y):
        y_groups = y.reshape(N_ROW, -1)

        def step_fn(accum, r):
            part = jax.vmap(dual_part, in_axes=(0, 0, 0, 0, None))(block_values[r], block_rows[r], block_cols[r], live_count[r], y_groups[r])
            return (accum + part.reshape(-1), None)
        accum, unused = lax.scan(step_fn, jnp.zeros((COLS,), jnp.float32), jnp.arange(N_ROW, dtype=jnp.int32))
        return accum

    def primal_total(extrap_low):
        x_groups = extrap_low.reshape(N_COL, -1)

        def step_fn(carry, r):
            part = jax.vmap(primal_part, in_axes=(0, 0, 0, 0, 0))(block_values[r], block_rows[r], block_cols[r], live_count[r], x_groups)
            return (carry, lax.optimization_barrier(jnp.sum(part, axis=0)))
        carry, stacked = lax.scan(step_fn, jnp.zeros((), jnp.float32), jnp.arange(N_ROW, dtype=jnp.int32))
        return stacked.reshape(-1)
    x = primal_start
    y = dual_start
    anchor_x = x
    anchor_y = y
    sum_x = jnp.zeros_like(x)
    sum_y = jnp.zeros_like(y)
    taken = jnp.zeros((), jnp.float32)
    omega = jnp.ones((), jnp.float32)
    for k in range(ITERS):
        step_primal = step_scale / omega
        step_dual = step_scale * omega
        dual_image = dual_total(y)
        x_next = jnp.minimum(jnp.maximum(x - step_primal * (objective - dual_image), 0.0), upper_bound)
        extrap_low = (2.0 * x_next - x).astype(jnp.bfloat16)
        primal_image = primal_total(extrap_low)
        y_next = jnp.maximum(y + step_dual * (demand - primal_image), 0.0)
        x = x_next
        y = y_next
        sum_x = sum_x + x
        sum_y = sum_y + y
        taken = taken + 1.0
        if k <= ITERS - 3:
            is_restart = restart_at[k] == 1
            mean_x = sum_x / taken
            mean_y = sum_y / taken
            drift_x = jnp.sum((mean_x - anchor_x) ** 2) / COLS + epsilon
            drift_y = jnp.sum((mean_y - anchor_y) ** 2) / ROWS + epsilon
            omega_next = jnp.sqrt(omega) * (drift_x / drift_y) ** 0.25
            x = jnp.where(is_restart, mean_x, x)
            y = jnp.where(is_restart, mean_y, y)
            anchor_x = jnp.where(is_restart, mean_x, anchor_x)
            anchor_y = jnp.where(is_restart, mean_y, anchor_y)
            sum_x = jnp.where(is_restart, jnp.zeros_like(sum_x), sum_x)
            sum_y = jnp.where(is_restart, jnp.zeros_like(sum_y), sum_y)
            taken = jnp.where(is_restart, jnp.zeros_like(taken), taken)
            omega = jnp.where(is_restart, omega_next, omega)
    return (x, y)
```

```python
import functools

import jax
import jax.numpy as jnp
from jax import lax
from jax.experimental import pallas as pl
from jax.experimental.pallas import tpu as pltpu
from jax.sharding import PartitionSpec as P

ITERS = 8
GROUP = 16
CHUNKS = 2

step_scale = 0.3
epsilon = 1e-06

MESH = pl.DeviceIdType.MESH


def fold(v):
    rows, lanes = v.shape
    v = jnp.sum(v.reshape(rows // 8, 8, lanes), axis=0)
    out = v[:, 0:128]
    for i in range(1, lanes // 128):
        out = out + v[:, 128 * i : 128 * (i + 1)]
    return out


def kernel(
    n_row,
    n_col,
    slots,
    block,
    k_hbm,
    idx_ref,
    restart_ref,
    obj_ref,
    ub_ref,
    dem_ref,
    x0_ref,
    y0_ref,
    xo_ref,
    yo_ref,
    k_v,
    ridx,
    cidx,
    oh_d,
    oh_p,
    oh_c,
    oh_r,
    drecv,
    precv,
    dyr,
    dxr,
    obj_s,
    ub_s,
    dem_s,
    x_s,
    y_s,
    ax_s,
    ay_s,
    sx_s,
    sy_s,
    ksem,
    is_r,
    ir_r,
    is_c,
    ir_c,
    ds_sem,
    dr_sem,
    ps_sem,
    pr_sem,
    ys_sem,
    yr_sem,
    xs_sem,
    xr_sem,
):
    me_r = lax.axis_index("row")
    me_c = lax.axis_index("col")
    col_blocks = x_s.shape[0]
    row_blocks = y_s.shape[0]
    total_cols = float(col_blocks * block * n_col)
    total_rows = float(row_blocks * block * n_row)
    bf16, f32 = jnp.bfloat16, jnp.float32
    groups = slots // GROUP
    per_chunk = slots // CHUNKS

    kcopies = []
    for g in range(groups):
        part = pl.ds(g * GROUP * block, GROUP * block)
        c = pltpu.make_async_copy(k_hbm.at[part, :], k_v.at[part, :], ksem.at[g])
        c.start()
        kcopies.append(c)

    row_peers = [lax.rem(me_r + d, n_row) for d in range(n_row - 1, 0, -1)]
    col_peers = [lax.rem(me_c + d, n_col) for d in range(n_col - 1, 0, -1)]

    barrier = pltpu.get_barrier_semaphore()
    for p in row_peers:
        pl.semaphore_signal(barrier, inc=1, device_id={"row": p}, device_id_type=MESH)
    for p in col_peers:
        pl.semaphore_signal(barrier, inc=1, device_id={"col": p}, device_id_type=MESH)

    half = block // 2

    def widen(ref, n):
        return jnp.concatenate(
            [ref[pl.ds(0, n, stride=2), :], ref[pl.ds(1, n, stride=2), :]], axis=1
        )

    obj_s[...] = widen(obj_ref, col_blocks)
    ub_s[...] = widen(ub_ref, col_blocks)
    dem_s[...] = widen(dem_ref, row_blocks)
    x_first = widen(x0_ref, col_blocks)
    y_first = widen(y0_ref, row_blocks)
    x_s[...] = x_first
    ax_s[...] = x_first
    sx_s[...] = jnp.zeros_like(x_first)
    y_s[...] = y_first
    ay_s[...] = y_first
    sy_s[...] = jnp.zeros_like(y_first)
    dyr[0, me_r] = jnp.zeros((8, 128), f32)
    dyr[1, me_r] = jnp.zeros((8, 128), f32)
    for c in range(n_col):
        dxr[1, c] = jnp.zeros((8, 128), f32)

    own_cols = idx_ref[0:1, :]
    own_rows = idx_ref[1:2, :]
    oh = (own_cols == lax.broadcasted_iota(jnp.int32, (col_blocks, 128), 0)).astype(f32)
    oh_c[...] = jnp.transpose(oh)[:slots, :].astype(bf16)
    pad = -(-row_blocks // 128) * 128
    oh = (own_rows == lax.broadcasted_iota(jnp.int32, (pad, 128), 0)).astype(f32)
    oh_r[...] = jnp.transpose(oh)[:slots, :row_blocks].astype(bf16)

    pl.semaphore_wait(barrier, n_row + n_col - 2)

    def remote(src, dst, ssem, rsem, axis, peer):
        return pltpu.make_async_remote_copy(
            src_ref=src,
            dst_ref=dst,
            send_sem=ssem,
            recv_sem=rsem,
            device_id={axis: peer},
            device_id_type=MESH,
        )

    ridx[me_r] = idx_ref[...]
    cidx[me_c] = idx_ref[...]
    for p in row_peers:
        remote(idx_ref, ridx.at[me_r], is_r.at[p], ir_r.at[me_r], "row", p).start()
    for p in col_peers:
        remote(idx_ref, cidx.at[me_c], is_c.at[p], ir_c.at[me_c], "col", p).start()
    for p in row_peers:
        remote(idx_ref, ridx.at[p], is_r.at[p], ir_r.at[p], "row", p).wait()
    for p in col_peers:
        remote(idx_ref, cidx.at[p], is_c.at[p], ir_c.at[p], "col", p).wait()

    every = jnp.concatenate([ridx[r][0:1, :slots] for r in range(n_row)], axis=1)
    oh_d[...] = (
        (every == lax.broadcasted_iota(jnp.int32, (col_blocks, n_row * slots), 0))
        .astype(f32)
        .astype(bf16)
    )
    every = jnp.concatenate([cidx[c][1:2, :slots] for c in range(n_col)], axis=1)
    oh_p[...] = (
        (every == lax.broadcasted_iota(jnp.int32, (row_blocks, n_col * slots), 0))
        .astype(f32)
        .astype(bf16)
    )
    for c in kcopies:
        c.wait()

    which = lax.broadcasted_iota(jnp.int32, (GROUP, block), 0)

    def spread(pieces, g):
        lhs = pieces[GROUP * g : GROUP * (g + 1), :]
        return [jnp.where(which == s, lhs, 0.0).astype(bf16) for s in range(GROUP)]

    def exchange_start(buf, ssem, rsem, par, me, axis, peers, ch):
        part = pl.ds(ch * per_chunk, per_chunk)
        src = buf.at[par, me, part, :]
        for p in peers:
            remote(src, src, ssem.at[par, p, ch], rsem.at[par, me, ch], axis, p).start()

    def exchange_wait(buf, ssem, rsem, par, axis, peers):
        for ch in range(CHUNKS):
            part = pl.ds(ch * per_chunk, per_chunk)
            for p in peers:
                dst = buf.at[par, p, part, :]
                remote(dst, dst, ssem.at[par, p, ch], rsem.at[par, p, ch], axis, p).wait()

    def tile_start(buf, ssem, rsem, par, me, axis, peers):
        src = buf.at[par, me]
        for p in peers:
            remote(src, src, ssem.at[par, p], rsem.at[par, me], axis, p).start()

    def tile_wait(buf, ssem, rsem, par, axis, peers):
        for p in peers:
            dst = buf.at[par, p]
            remote(dst, dst, ssem.at[par, p], rsem.at[par, p], axis, p).wait()

    def total(buf, par, n):
        acc = buf[par, 0]
        for i in range(1, n):
            acc = acc + buf[par, i]
        acc = jnp.sum(acc, axis=0, keepdims=True)
        return jnp.sum(acc, axis=1, keepdims=True)

    def body(k, carry):
        omega, taken = carry
        par = lax.rem(k, 2)
        old = lax.rem(k + 1, 2)
        flag_now = jnp.where(k <= ITERS - 3, restart_ref[k], 0) == 1
        flag_old = (
            jnp.where((k >= 1) & (k <= ITERS - 2), restart_ref[jnp.maximum(k - 1, 0)], 0) == 1
        )

        tile_start(dyr, ys_sem, yr_sem, par, me_r, "row", row_peers)
        y_low = y_s[...].astype(bf16)
        pieces = jnp.dot(oh_r[...], y_low, preferred_element_type=f32)
        for g in range(groups):
            lhs = jnp.concatenate(spread(pieces, g), axis=1)
            prod = jnp.dot(
                lhs,
                k_v[pl.ds(g * GROUP * block, GROUP * block), :],
                preferred_element_type=f32,
            )
            drecv[par, me_r, pl.ds(g * GROUP, GROUP), :] = prod.astype(bf16)
            if (g + 1) * GROUP % per_chunk == 0:
                exchange_start(
                    drecv, ds_sem, dr_sem, par, me_r, "row", row_peers,
                    (g + 1) * GROUP // per_chunk - 1,
                )
        tile_wait(dyr, ys_sem, yr_sem, par, "row", row_peers)
        drift_x = total(dxr, old, n_col) / total_cols + epsilon
        drift_y = total(dyr, par, n_row) / total_rows + epsilon
        omega_next = jnp.sqrt(omega) * jnp.sqrt(jnp.sqrt(drift_x / drift_y))
        omega = jnp.where(flag_old, omega_next, omega)
        tau = step_scale / omega
        sigma = step_scale * omega

        exchange_wait(drecv, ds_sem, dr_sem, par, "row", row_peers)
        dual = jnp.dot(
            oh_d[...],
            drecv[par].reshape(n_row * slots, block),
            preferred_element_type=f32,
        )
        x = x_s[...]
        x_next = jnp.minimum(jnp.maximum(x - tau * (obj_s[...] - dual), 0.0), ub_s[...])
        extrap = (2.0 * x_next - x).astype(bf16)
        pieces = jnp.dot(oh_c[...], extrap, preferred_element_type=f32)

        taken = taken + 1.0
        inv = 1.0 / taken
        sum_x = sx_s[...] + x_next
        mean_x = sum_x * inv
        gap = mean_x - ax_s[...]
        dxr[par, me_c] = fold(gap * gap)
        tile_start(dxr, xs_sem, xr_sem, par, me_c, "col", col_peers)
        x_s[...] = jnp.where(flag_now, mean_x, x_next)
        ax_s[...] = jnp.where(flag_now, mean_x, ax_s[...])
        sx_s[...] = jnp.where(flag_now, 0.0, sum_x)

        for g in range(groups):
            prod = None
            for s, lhs in enumerate(spread(pieces, g)):
                term = lax.dot_general(
                    lhs,
                    k_v[pl.ds((g * GROUP + s) * block, block), :],
                    (((1,), (1,)), ((), ())),
                    preferred_element_type=f32,
                )
                prod = term if prod is None else prod + term
            precv[par, me_c, pl.ds(g * GROUP, GROUP), :] = prod.astype(bf16)
            if (g + 1) * GROUP % per_chunk == 0:
                exchange_start(
                    precv, ps_sem, pr_sem, par, me_c, "col", col_peers,
                    (g + 1) * GROUP // per_chunk - 1,
                )
        tile_wait(dxr, xs_sem, xr_sem, par, "col", col_peers)
        exchange_wait(precv, ps_sem, pr_sem, par, "col", col_peers)
        primal = jnp.dot(
            oh_p[...],
            precv[par].reshape(n_col * slots, block),
            preferred_element_type=f32,
        )
        y_next = jnp.maximum(y_s[...] + sigma * (dem_s[...] - primal), 0.0)
        sum_y = sy_s[...] + y_next
        mean_y = sum_y * inv
        gap = mean_y - ay_s[...]
        dyr[old, me_r] = fold(gap * gap)
        y_s[...] = jnp.where(flag_now, mean_y, y_next)
        ay_s[...] = jnp.where(flag_now, mean_y, ay_s[...])
        sy_s[...] = jnp.where(flag_now, 0.0, sum_y)
        taken = jnp.where(flag_now, 0.0, taken)
        return omega, taken

    one = jnp.ones((1, 1), f32)
    lax.fori_loop(0, ITERS, body, (one, jnp.zeros((1, 1), f32)))
    xo_ref[pl.ds(0, col_blocks, stride=2), :] = x_s[:, :half]
    xo_ref[pl.ds(1, col_blocks, stride=2), :] = x_s[:, half:]
    yo_ref[pl.ds(0, row_blocks, stride=2), :] = y_s[:, :half]
    yo_ref[pl.ds(1, row_blocks, stride=2), :] = y_s[:, half:]


def shards(
    block_values,
    block_rows,
    block_cols,
    live_count,
    objective,
    upper_bound,
    demand,
    primal_start,
    dual_start,
    restart_at,
):
    slots, block = block_values.shape[2], block_values.shape[3]
    n_row = lax.axis_size("row")
    n_col = lax.axis_size("col")
    row_blocks = demand.shape[0] // block
    col_blocks = objective.shape[0] // block
    live = jnp.arange(slots, dtype=jnp.int32) < live_count[0, 0]
    index = jnp.stack([block_cols[0, 0], block_rows[0, 0]])
    index = jnp.where(live[None, :], index, -1)
    index = jnp.pad(index, ((0, 6), (0, 128 - slots)), constant_values=-1)
    wide = lambda v: v.reshape(-1, 128)
    f32, bf16 = jnp.float32, jnp.bfloat16
    vmem = pl.BlockSpec(memory_space=pltpu.VMEM)
    dma = pltpu.SemaphoreType.DMA
    x_shape, y_shape = (col_blocks, block), (row_blocks, block)
    x_out, y_out = pl.pallas_call(
        functools.partial(kernel, n_row, n_col, slots, block),
        out_shape=(
            jax.ShapeDtypeStruct((col_blocks * block // 128, 128), f32),
            jax.ShapeDtypeStruct((row_blocks * block // 128, 128), f32),
        ),
        in_specs=[
            pl.BlockSpec(memory_space=pl.ANY),
            vmem,
            pl.BlockSpec(memory_space=pltpu.SMEM),
            vmem,
            vmem,
            vmem,
            vmem,
            vmem,
        ],
        out_specs=(vmem, vmem),
        scratch_shapes=[
            pltpu.VMEM((slots * block, block), bf16),
            pltpu.VMEM((n_row, 8, 128), jnp.int32),
            pltpu.VMEM((n_col, 8, 128), jnp.int32),
            pltpu.VMEM((col_blocks, n_row * slots), bf16),
            pltpu.VMEM((row_blocks, n_col * slots), bf16),
            pltpu.VMEM((slots, col_blocks), bf16),
            pltpu.VMEM((slots, row_blocks), bf16),
            pltpu.VMEM((2, n_row, slots, block), bf16),
            pltpu.VMEM((2, n_col, slots, block), bf16),
            pltpu.VMEM((2, n_row, 8, 128), f32),
            pltpu.VMEM((2, n_col, 8, 128), f32),
            pltpu.VMEM(x_shape, f32),
            pltpu.VMEM(x_shape, f32),
            pltpu.VMEM(y_shape, f32),
            pltpu.VMEM(x_shape, f32),
            pltpu.VMEM(y_shape, f32),
            pltpu.VMEM(x_shape, f32),
            pltpu.VMEM(y_shape, f32),
            pltpu.VMEM(x_shape, f32),
            pltpu.VMEM(y_shape, f32),
            dma((slots // GROUP,)),
            dma((n_row,)),
            dma((n_row,)),
            dma((n_col,)),
            dma((n_col,)),
            dma((2, n_row, CHUNKS)),
            dma((2, n_row, CHUNKS)),
            dma((2, n_col, CHUNKS)),
            dma((2, n_col, CHUNKS)),
            dma((2, n_row)),
            dma((2, n_row)),
            dma((2, n_col)),
            dma((2, n_col)),
        ],
        compiler_params=pltpu.CompilerParams(collective_id=0, has_side_effects=True),
    )(
        block_values.reshape(slots * block, block),
        index,
        restart_at,
        wide(objective),
        wide(upper_bound),
        wide(demand),
        wide(primal_start),
        wide(dual_start),
    )
    return x_out.reshape(-1), y_out.reshape(-1)


def solution(mesh):
    placed = (
        P("row", "col", None, None, None),
        P("row", "col", None),
        P("row", "col", None),
        P("row", "col"),
        P("col"),
        P("col"),
        P("row"),
        P("col"),
        P("row"),
        P(),
    )
    return jax.shard_map(
        shards, mesh=mesh, in_specs=placed, out_specs=(P("col"), P("row")), check_vma=False
    )
```

```python
import functools

import jax
import jax.numpy as jnp
from jax import lax
from jax.experimental import pallas as pl
from jax.experimental.pallas import tpu as pltpu
from jax.sharding import PartitionSpec as P

ITERS = 8
GROUP = 16
SPLIT = 2

step_scale = 0.3
epsilon = 1e-06

MESH = pl.DeviceIdType.MESH


def fold(v):
    rows, lanes = v.shape
    v = jnp.sum(v.reshape(rows // 8, 8, lanes), axis=0)
    out = v[:, 0:128]
    for i in range(1, lanes // 128):
        out = out + v[:, 128 * i : 128 * (i + 1)]
    return out


def peers_of(me, n):
    if n & (n - 1):
        return [lax.rem(me + d, n) for d in range(n - 1, 0, -1)]
    out = []
    for m in sorted(range(1, n), key=lambda m: (-(m // 2).bit_count(), m)):
        p = me
        bit = 1
        while bit < n:
            if m & bit:
                p = p + bit - 2 * bit * lax.rem(lax.div(me, bit), 2)
            bit *= 2
        out.append(p)
    return out


def kernel(
    n_row,
    n_col,
    slots,
    block,
    k_hbm,
    cols_ref,
    rows_ref,
    live_ref,
    restart_ref,
    obj_hbm,
    ub_hbm,
    dem_hbm,
    x0_hbm,
    y0_hbm,
    xo_hbm,
    yo_hbm,
    k_v,
    kt_v,
    idx,
    ridx,
    cidx,
    oh_d,
    oh_p,
    oh_c,
    oh_r,
    drecv,
    precv,
    dyr,
    dxr,
    raw_x,
    raw_y,
    obj_s,
    ub_s,
    dem_s,
    x_s,
    y_s,
    ax_s,
    ay_s,
    sx_s,
    sy_s,
    ksem,
    rawsem,
    outsem,
    is_r,
    ir_r,
    is_c,
    ir_c,
    ds_sem,
    dr_sem,
    ps_sem,
    pr_sem,
    ys_sem,
    yr_sem,
    xs_sem,
    xr_sem,
):
    me_r = lax.axis_index("row")
    me_c = lax.axis_index("col")
    col_blocks = x_s.shape[0]
    row_blocks = y_s.shape[0]
    total_cols = float(col_blocks * block * n_col)
    total_rows = float(row_blocks * block * n_row)
    bf16, f32 = jnp.bfloat16, jnp.float32
    groups = slots // GROUP
    half = block // 2
    chunks = ((0, SPLIT * GROUP), (SPLIT * GROUP, slots - SPLIT * GROUP))

    row_peers = peers_of(me_r, n_row)
    col_peers = peers_of(me_c, n_col)
    barrier = pltpu.get_barrier_semaphore()
    for p in row_peers:
        pl.semaphore_signal(barrier, inc=1, device_id={"row": p}, device_id_type=MESH)
    for p in col_peers:
        pl.semaphore_signal(barrier, inc=1, device_id={"col": p}, device_id_type=MESH)

    y_in = pltpu.make_async_copy(y0_hbm, raw_y.at[0], rawsem.at[0])
    y_in.start()
    kcopies = []
    for g in range(groups):
        part = pl.ds(g * GROUP * block, GROUP * block)
        c = pltpu.make_async_copy(k_hbm.at[part, :], k_v.at[part, :], ksem.at[g])
        c.start()
        kcopies.append(c)
    ins = [
        pltpu.make_async_copy(dem_hbm, raw_y.at[1], rawsem.at[1]),
        pltpu.make_async_copy(x0_hbm, raw_x.at[0], rawsem.at[2]),
        pltpu.make_async_copy(obj_hbm, raw_x.at[1], rawsem.at[3]),
        pltpu.make_async_copy(ub_hbm, raw_x.at[2], rawsem.at[4]),
    ]
    for c in ins:
        c.start()
    out_x = pltpu.make_async_copy(raw_x.at[0], xo_hbm, outsem.at[0])
    out_y = pltpu.make_async_copy(raw_y.at[0], yo_hbm, outsem.at[1])

    def widen(ref, at, n):
        return jnp.concatenate(
            [ref[at, pl.ds(0, n, stride=2), :], ref[at, pl.ds(1, n, stride=2), :]], axis=1
        )

    def narrow(ref, value, n):
        ref[0, pl.ds(0, n, stride=2), :] = value[:, :half]
        ref[0, pl.ds(1, n, stride=2), :] = value[:, half:]

    live = lax.broadcasted_iota(jnp.int32, (1, slots), 1) < live_ref[0, 0]
    idx[...] = jnp.full((8, 128), -1, jnp.int32)
    idx[0:1, :slots] = jnp.where(live, cols_ref[...], -1)
    idx[1:2, :slots] = jnp.where(live, rows_ref[...], -1)
    own = idx[...]
    oh = (own[0:1, :] == lax.broadcasted_iota(jnp.int32, (col_blocks, 128), 0)).astype(f32)
    oh_c[...] = jnp.transpose(oh)[:slots, :].astype(bf16)
    pad = -(-row_blocks // 128) * 128
    oh = (own[1:2, :] == lax.broadcasted_iota(jnp.int32, (pad, 128), 0)).astype(f32)
    oh_r[...] = jnp.transpose(oh)[:slots, :row_blocks].astype(bf16)
    ridx[me_r] = own
    cidx[me_c] = own
    dyr[0, me_r] = jnp.zeros((8, 128), f32)
    dyr[1, me_r] = jnp.zeros((8, 128), f32)
    for c in range(n_col):
        dxr[1, c] = jnp.zeros((8, 128), f32)

    y_in.wait()
    y_first = widen(raw_y, 0, row_blocks)
    y_s[...] = y_first
    ay_s[...] = y_first
    sy_s[...] = jnp.zeros_like(y_first)

    pl.semaphore_wait(barrier, n_row + n_col - 2)

    def remote(src, dst, ssem, rsem, axis, peer):
        return pltpu.make_async_remote_copy(
            src_ref=src,
            dst_ref=dst,
            send_sem=ssem,
            recv_sem=rsem,
            device_id={axis: peer},
            device_id_type=MESH,
        )

    for p in row_peers:
        remote(idx, ridx.at[me_r], is_r.at[p], ir_r.at[me_r], "row", p).start()
    for p in col_peers:
        remote(idx, cidx.at[me_c], is_c.at[p], ir_c.at[me_c], "col", p).start()

    def settle():
        for c in ins:
            c.wait()
        dem_s[...] = widen(raw_y, 1, row_blocks)
        obj_s[...] = widen(raw_x, 1, col_blocks)
        ub_s[...] = widen(raw_x, 2, col_blocks)
        x_first = widen(raw_x, 0, col_blocks)
        x_s[...] = x_first
        ax_s[...] = x_first
        sx_s[...] = jnp.zeros_like(x_first)

        def turn(t, carry):
            for u in range(4):
                part = pl.ds(pl.multiple_of((t * 4 + u) * block, block), block)
                kt_v[part, :] = jnp.transpose(k_v[part, :])
            return carry

        lax.fori_loop(0, slots // 4, turn, 0)
        for p in row_peers:
            remote(idx, ridx.at[p], is_r.at[p], ir_r.at[p], "row", p).wait()
        for p in col_peers:
            remote(idx, cidx.at[p], is_c.at[p], ir_c.at[p], "col", p).wait()
        every = jnp.concatenate([ridx[r][0:1, :slots] for r in range(n_row)], axis=1)
        oh_d[...] = (
            (every == lax.broadcasted_iota(jnp.int32, (col_blocks, n_row * slots), 0))
            .astype(f32)
            .astype(bf16)
        )
        every = jnp.concatenate([cidx[c][1:2, :slots] for c in range(n_col)], axis=1)
        oh_p[...] = (
            (every == lax.broadcasted_iota(jnp.int32, (row_blocks, n_col * slots), 0))
            .astype(f32)
            .astype(bf16)
        )

    which = lax.broadcasted_iota(jnp.int32, (GROUP, block), 0)

    def exchange(buf, ssem, rsem, par, me, axis, peers, ch, act):
        part = pl.ds(*chunks[ch])
        if act == "start":
            src = buf.at[par, me, part, :]
            for p in peers:
                remote(src, src, ssem.at[par, p, ch], rsem.at[par, me, ch], axis, p).start()
            return
        for p in peers:
            dst = buf.at[par, p, part, :]
            c = remote(dst, dst, ssem.at[par, p, ch], rsem.at[par, p, ch], axis, p)
            c.wait_recv() if act == "recv" else c.wait_send()

    def tile(buf, ssem, rsem, par, me, axis, peers, act):
        if act == "start":
            src = buf.at[par, me]
            for p in peers:
                remote(src, src, ssem.at[par, p], rsem.at[par, me], axis, p).start()
            return
        for p in peers:
            dst = buf.at[par, p]
            remote(dst, dst, ssem.at[par, p], rsem.at[par, p], axis, p).wait()

    def both(*args):
        exchange(*args[:-1], 0, args[-1])
        exchange(*args[:-1], 1, args[-1])

    def products(pieces, mat, buf, me, par, args, first):
        for g in range(groups):
            if first:
                kcopies[g].wait()
            part = pieces[GROUP * g : GROUP * (g + 1), :]
            lhs = jnp.concatenate(
                [jnp.where(which == s, part, 0.0).astype(bf16) for s in range(GROUP)], axis=1
            )
            prod = jnp.dot(
                lhs,
                mat[pl.ds(g * GROUP * block, GROUP * block), :],
                preferred_element_type=f32,
            )
            buf[par, me, pl.ds(g * GROUP, GROUP), :] = prod.astype(bf16)
            if g + 1 == SPLIT:
                exchange(*args, 0, "start")
        exchange(*args, 1, "start")

    def total(buf, par, n):
        acc = buf[par, 0]
        for i in range(1, n):
            acc = acc + buf[par, i]
        acc = jnp.sum(acc, axis=0, keepdims=True)
        return jnp.sum(acc, axis=1, keepdims=True)

    def body(k, carry, first=False):
        omega, taken = carry
        par = lax.rem(k, 2)
        old = lax.rem(k + 1, 2)
        d_args = (drecv, ds_sem, dr_sem, par, me_r, "row", row_peers)
        p_args = (precv, ps_sem, pr_sem, par, me_c, "col", col_peers)
        flag_now = jnp.where(k <= ITERS - 3, restart_ref[k], 0) == 1

        if not first:
            tile(dyr, ys_sem, yr_sem, par, me_r, "row", row_peers, "start")
        y_low = y_s[...].astype(bf16)
        pieces = jnp.dot(oh_r[...], y_low, preferred_element_type=f32)
        products(pieces, k_v, drecv, me_r, par, d_args, first)
        if first:
            settle()
        else:
            both(precv, ps_sem, pr_sem, old, me_c, "col", col_peers, "sent")
            flag_old = jnp.where(k <= ITERS - 2, restart_ref[k - 1], 0) == 1
            tile(dyr, ys_sem, yr_sem, par, me_r, "row", row_peers, "wait")
            drift_x = total(dxr, old, n_col) / total_cols + epsilon
            drift_y = total(dyr, par, n_row) / total_rows + epsilon
            omega_next = jnp.sqrt(omega) * jnp.sqrt(jnp.sqrt(drift_x / drift_y))
            omega = jnp.where(flag_old, omega_next, omega)
        tau = step_scale / omega
        sigma = step_scale * omega

        both(*d_args, "recv")
        dual = jnp.dot(
            oh_d[...],
            drecv[par].reshape(n_row * slots, block),
            preferred_element_type=f32,
        )
        x = x_s[...]
        x_next = jnp.minimum(jnp.maximum(x - tau * (obj_s[...] - dual), 0.0), ub_s[...])
        extrap = (2.0 * x_next - x).astype(bf16)
        pieces = jnp.dot(oh_c[...], extrap, preferred_element_type=f32)
        x_s[...] = x_next
        products(pieces, kt_v, precv, me_c, par, p_args, False)

        x_next = x_s[...]
        taken = taken + 1.0
        inv = 1.0 / taken
        sum_x = sx_s[...] + x_next
        mean_x = sum_x * inv
        gap = mean_x - ax_s[...]
        dxr[par, me_c] = fold(gap * gap)
        tile(dxr, xs_sem, xr_sem, par, me_c, "col", col_peers, "start")
        x_last = jnp.where(flag_now, mean_x, x_next)
        x_s[...] = x_last
        ax_s[...] = jnp.where(flag_now, mean_x, ax_s[...])
        sx_s[...] = jnp.where(flag_now, 0.0, sum_x)
        both(*d_args, "sent")
        if not first:

            @pl.when(k == ITERS - 1)
            def _():
                narrow(raw_x, x_s[...], col_blocks)
                out_x.start()

        both(*p_args, "recv")
        primal = jnp.dot(
            oh_p[...],
            precv[par].reshape(n_col * slots, block),
            preferred_element_type=f32,
        )
        y_next = jnp.maximum(y_s[...] + sigma * (dem_s[...] - primal), 0.0)
        sum_y = sy_s[...] + y_next
        mean_y = sum_y * inv
        gap = mean_y - ay_s[...]
        dyr[old, me_r] = fold(gap * gap)
        y_s[...] = jnp.where(flag_now, mean_y, y_next)
        ay_s[...] = jnp.where(flag_now, mean_y, ay_s[...])
        sy_s[...] = jnp.where(flag_now, 0.0, sum_y)
        taken = jnp.where(flag_now, 0.0, taken)
        tile(dxr, xs_sem, xr_sem, par, me_c, "col", col_peers, "wait")
        return omega, taken

    carry = body(0, (jnp.ones((1, 1), f32), jnp.zeros((1, 1), f32)), True)
    lax.fori_loop(1, ITERS, body, carry)
    narrow(raw_y, y_s[...], row_blocks)
    out_y.start()
    both(precv, ps_sem, pr_sem, (ITERS - 1) % 2, me_c, "col", col_peers, "sent")
    out_x.wait()
    out_y.wait()


def shards(
    block_values,
    block_rows,
    block_cols,
    live_count,
    objective,
    upper_bound,
    demand,
    primal_start,
    dual_start,
    restart_at,
):
    slots, block = block_values.shape[2], block_values.shape[3]
    n_row = lax.axis_size("row")
    n_col = lax.axis_size("col")
    row_blocks = demand.shape[0] // block
    col_blocks = objective.shape[0] // block
    wide = lambda v: v.reshape(-1, 128)
    f32, bf16 = jnp.float32, jnp.bfloat16
    vmem = pl.BlockSpec(memory_space=pltpu.VMEM)
    smem = pl.BlockSpec(memory_space=pltpu.SMEM)
    hbm = pl.BlockSpec(memory_space=pl.ANY)
    dma = pltpu.SemaphoreType.DMA
    x_shape, y_shape = (col_blocks, block), (row_blocks, block)
    x_out, y_out = pl.pallas_call(
        functools.partial(kernel, n_row, n_col, slots, block),
        out_shape=(
            jax.ShapeDtypeStruct((col_blocks * block // 128, 128), f32),
            jax.ShapeDtypeStruct((row_blocks * block // 128, 128), f32),
        ),
        in_specs=[
            hbm,
            vmem,
            vmem,
            smem,
            smem,
            hbm,
            hbm,
            hbm,
            hbm,
            hbm,
        ],
        out_specs=(hbm, hbm),
        scratch_shapes=[
            pltpu.VMEM((slots * block, block), bf16),
            pltpu.VMEM((slots * block, block), bf16),
            pltpu.VMEM((8, 128), jnp.int32),
            pltpu.VMEM((n_row, 8, 128), jnp.int32),
            pltpu.VMEM((n_col, 8, 128), jnp.int32),
            pltpu.VMEM((col_blocks, n_row * slots), bf16),
            pltpu.VMEM((row_blocks, n_col * slots), bf16),
            pltpu.VMEM((slots, col_blocks), bf16),
            pltpu.VMEM((slots, row_blocks), bf16),
            pltpu.VMEM((2, n_row, slots, block), bf16),
            pltpu.VMEM((2, n_col, slots, block), bf16),
            pltpu.VMEM((2, n_row, 8, 128), f32),
            pltpu.VMEM((2, n_col, 8, 128), f32),
            pltpu.VMEM((3, col_blocks * block // 128, 128), f32),
            pltpu.VMEM((2, row_blocks * block // 128, 128), f32),
            pltpu.VMEM(x_shape, f32),
            pltpu.VMEM(x_shape, f32),
            pltpu.VMEM(y_shape, f32),
            pltpu.VMEM(x_shape, f32),
            pltpu.VMEM(y_shape, f32),
            pltpu.VMEM(x_shape, f32),
            pltpu.VMEM(y_shape, f32),
            pltpu.VMEM(x_shape, f32),
            pltpu.VMEM(y_shape, f32),
            dma((slots // GROUP,)),
            dma((5,)),
            dma((2,)),
            dma((n_row,)),
            dma((n_row,)),
            dma((n_col,)),
            dma((n_col,)),
            dma((2, n_row, 2)),
            dma((2, n_row, 2)),
            dma((2, n_col, 2)),
            dma((2, n_col, 2)),
            dma((2, n_row)),
            dma((2, n_row)),
            dma((2, n_col)),
            dma((2, n_col)),
        ],
        compiler_params=pltpu.CompilerParams(collective_id=0, has_side_effects=True),
    )(
        block_values.reshape(slots * block, block),
        block_cols[0],
        block_rows[0],
        live_count,
        restart_at,
        wide(objective),
        wide(upper_bound),
        wide(demand),
        wide(primal_start),
        wide(dual_start),
    )
    return x_out.reshape(-1), y_out.reshape(-1)


def solution(mesh):
    placed = (
        P("row", "col", None, None, None),
        P("row", "col", None),
        P("row", "col", None),
        P("row", "col"),
        P("col"),
        P("col"),
        P("row"),
        P("col"),
        P("row"),
        P(),
    )
    return jax.shard_map(
        shards, mesh=mesh, in_specs=placed, out_specs=(P("col"), P("row")), check_vma=False
    )
```

```python
import functools

import jax
import jax.numpy as jnp
from jax import lax
from jax.experimental import pallas as pl
from jax.experimental.pallas import tpu as pltpu
from jax.sharding import PartitionSpec as P

ITERS = 8
GROUP = 16

step_scale = 0.3
epsilon = 1e-06

MESH = pl.DeviceIdType.MESH


def fold(v):
    rows, lanes = v.shape
    v = jnp.sum(v.reshape(rows // 8, 8, lanes), axis=0)
    out = v[:, 0:128]
    for i in range(1, lanes // 128):
        out = out + v[:, 128 * i : 128 * (i + 1)]
    return jnp.sum(out, axis=0, keepdims=True)


def peers_of(me, n):
    if n & (n - 1):
        return [lax.rem(me + d, n) for d in range(n - 1, 0, -1)]
    out = []
    for m in sorted(range(1, n), key=lambda m: (-(m // 2).bit_count(), m)):
        p = me
        bit = 1
        while bit < n:
            if m & bit:
                p = p + bit - 2 * bit * lax.rem(lax.div(me, bit), 2)
            bit *= 2
        out.append(p)
    return out


def kernel(
    n_row,
    n_col,
    slots,
    block,
    k_hbm,
    cols_ref,
    rows_ref,
    live_ref,
    restart_ref,
    obj_hbm,
    ub_hbm,
    dem_hbm,
    x0_hbm,
    y0_hbm,
    xo_hbm,
    yo_hbm,
    k_v,
    kt_v,
    idx,
    ridx,
    cidx,
    oh_d,
    oh_p,
    oh_c,
    oh_r,
    drecv,
    precv,
    dyr,
    dxr,
    raw_x,
    raw_y,
    obj_s,
    ub_s,
    dem_s,
    x_s,
    y_s,
    ax_s,
    ay_s,
    sx_s,
    sy_s,
    ksem,
    rawsem,
    outsem,
    is_r,
    ir_r,
    is_c,
    ir_c,
    ds_sem,
    dr_sem,
    ps_sem,
    pr_sem,
    ys_sem,
    yr_sem,
    xs_sem,
    xr_sem,
):
    me_r = lax.axis_index("row")
    me_c = lax.axis_index("col")
    col_blocks = x_s.shape[0]
    row_blocks = y_s.shape[0]
    total_cols = float(col_blocks * block * n_col)
    total_rows = float(row_blocks * block * n_row)
    bf16, f32 = jnp.bfloat16, jnp.float32
    groups = slots // GROUP
    half = block // 2
    split = groups // 2
    part_slots = slots // 2

    row_peers = peers_of(me_r, n_row)
    col_peers = peers_of(me_c, n_col)
    barrier = pltpu.get_barrier_semaphore()
    for p in row_peers:
        pl.semaphore_signal(barrier, inc=1, device_id={"row": p}, device_id_type=MESH)
    for p in col_peers:
        pl.semaphore_signal(barrier, inc=1, device_id={"col": p}, device_id_type=MESH)

    y_in = pltpu.make_async_copy(y0_hbm, raw_y.at[0], rawsem.at[0])
    y_in.start()
    kcopies = []
    for g in range(groups):
        part = pl.ds(g * GROUP * block, GROUP * block)
        c = pltpu.make_async_copy(k_hbm.at[part, :], k_v.at[part, :], ksem.at[g])
        c.start()
        kcopies.append(c)
    ins = [
        pltpu.make_async_copy(dem_hbm, raw_y.at[1], rawsem.at[1]),
        pltpu.make_async_copy(x0_hbm, raw_x.at[0], rawsem.at[2]),
        pltpu.make_async_copy(obj_hbm, raw_x.at[1], rawsem.at[3]),
        pltpu.make_async_copy(ub_hbm, raw_x.at[2], rawsem.at[4]),
    ]
    for c in ins:
        c.start()
    out_x = pltpu.make_async_copy(raw_x.at[0], xo_hbm, outsem.at[0])
    out_y = pltpu.make_async_copy(raw_y.at[0], yo_hbm, outsem.at[1])

    def widen(ref, at, n):
        return jnp.concatenate(
            [ref[at, pl.ds(0, n, stride=2), :], ref[at, pl.ds(1, n, stride=2), :]], axis=1
        )

    def narrow(ref, value, n):
        ref[0, pl.ds(0, n, stride=2), :] = value[:, :half]
        ref[0, pl.ds(1, n, stride=2), :] = value[:, half:]

    live = lax.broadcasted_iota(jnp.int32, (1, slots), 1) < live_ref[0, 0]
    idx[...] = jnp.full((8, 128), -1, jnp.int32)
    idx[0:1, :slots] = jnp.where(live, cols_ref[...], -1)
    idx[1:2, :slots] = jnp.where(live, rows_ref[...], -1)
    own = idx[...]
    oh = (own[0:1, :] == lax.broadcasted_iota(jnp.int32, (col_blocks, 128), 0)).astype(f32)
    oh_c[...] = jnp.transpose(oh)[:slots, :].astype(bf16)
    pad = -(-row_blocks // 128) * 128
    oh = (own[1:2, :] == lax.broadcasted_iota(jnp.int32, (pad, 128), 0)).astype(f32)
    oh_r[...] = jnp.transpose(oh)[:slots, :row_blocks].astype(bf16)
    ridx[me_r] = own
    cidx[me_c] = own
    dyr[0, me_r] = jnp.zeros((1, 128), f32)
    dyr[1, me_r] = jnp.zeros((1, 128), f32)
    for c in range(n_col):
        dxr[1, c] = jnp.zeros((1, 128), f32)

    y_in.wait()
    y_first = widen(raw_y, 0, row_blocks)
    y_s[...] = y_first
    ay_s[...] = y_first
    sy_s[...] = jnp.zeros_like(y_first)

    pl.semaphore_wait(barrier, n_row + n_col - 2)

    def remote(src, dst, ssem, rsem, axis, peer):
        return pltpu.make_async_remote_copy(
            src_ref=src,
            dst_ref=dst,
            send_sem=ssem,
            recv_sem=rsem,
            device_id={axis: peer},
            device_id_type=MESH,
        )

    for p in row_peers:
        remote(idx, ridx.at[me_r], is_r.at[p], ir_r.at[me_r], "row", p).start()
    for p in col_peers:
        remote(idx, cidx.at[me_c], is_c.at[p], ir_c.at[me_c], "col", p).start()

    def settle():
        for c in ins:
            c.wait()
        dem_s[...] = widen(raw_y, 1, row_blocks)
        obj_s[...] = widen(raw_x, 1, col_blocks)
        ub_s[...] = widen(raw_x, 2, col_blocks)
        x_first = widen(raw_x, 0, col_blocks)
        x_s[...] = x_first
        ax_s[...] = x_first
        sx_s[...] = jnp.zeros_like(x_first)

        def turn(t, carry):
            for u in range(4):
                part = pl.ds(pl.multiple_of((t * 4 + u) * block, block), block)
                kt_v[part, :] = jnp.transpose(k_v[part, :])
            return carry

        lax.fori_loop(0, slots // 4, turn, 0)
        for p in row_peers:
            remote(idx, ridx.at[p], is_r.at[p], ir_r.at[p], "row", p).wait()
        for p in col_peers:
            remote(idx, cidx.at[p], is_c.at[p], ir_c.at[p], "col", p).wait()
        for ch in range(2):
            lanes = slice(ch * part_slots, (ch + 1) * part_slots)
            every = jnp.concatenate([ridx[r][0:1, lanes] for r in range(n_row)], axis=1)
            at = lax.broadcasted_iota(jnp.int32, (col_blocks, n_row * part_slots), 0)
            oh_d[ch] = (every == at).astype(f32).astype(bf16)
            every = jnp.concatenate([cidx[c][1:2, lanes] for c in range(n_col)], axis=1)
            at = lax.broadcasted_iota(jnp.int32, (row_blocks, n_col * part_slots), 0)
            oh_p[ch] = (every == at).astype(f32).astype(bf16)

    which = lax.broadcasted_iota(jnp.int32, (GROUP, block), 0)

    def exchange(buf, ssem, rsem, par, me, axis, peers, ch, act):
        if act == "start":
            src = buf.at[par, ch, me]
            for p in peers:
                remote(src, src, ssem.at[par, p, ch], rsem.at[par, me, ch], axis, p).start()
            return
        for p in peers:
            dst = buf.at[par, ch, p]
            c = remote(dst, dst, ssem.at[par, p, ch], rsem.at[par, p, ch], axis, p)
            c.wait_recv() if act == "recv" else c.wait_send()

    def tile(buf, ssem, rsem, par, me, axis, peers, act):
        if act == "start":
            src = buf.at[par, me]
            for p in peers:
                remote(src, src, ssem.at[par, p], rsem.at[par, me], axis, p).start()
            return
        for p in peers:
            dst = buf.at[par, p]
            remote(dst, dst, ssem.at[par, p], rsem.at[par, p], axis, p).wait()

    def both(*args):
        exchange(*args[:-1], 0, args[-1])
        exchange(*args[:-1], 1, args[-1])

    def products(pieces, mat, buf, me, par, args, first):
        for g in range(groups):
            if first:
                kcopies[g].wait()
            part = pieces[GROUP * g : GROUP * (g + 1), :]
            lhs = jnp.concatenate(
                [jnp.where(which == s, part, 0.0).astype(bf16) for s in range(GROUP)], axis=1
            )
            prod = jnp.dot(
                lhs,
                mat[pl.ds(g * GROUP * block, GROUP * block), :],
                preferred_element_type=f32,
            )
            buf[par, g // split, me, pl.ds(g % split * GROUP, GROUP), :] = prod.astype(bf16)
            if g + 1 == split:
                exchange(*args, 0, "start")
        exchange(*args, 1, "start")

    def gather_sum(oh, args, n):
        acc = None
        for ch in range(2):
            exchange(*args, ch, "recv")
            term = jnp.dot(
                oh[ch],
                args[0][args[3], ch].reshape(n * part_slots, block),
                preferred_element_type=f32,
            )
            acc = term if acc is None else acc + term
        return acc

    def total(buf, par, n):
        acc = buf[par, 0]
        for i in range(1, n):
            acc = acc + buf[par, i]
        acc = jnp.sum(acc, axis=0, keepdims=True)
        return jnp.sum(acc, axis=1, keepdims=True)

    def body(k, carry, first=False):
        omega, taken = carry
        par = lax.rem(k, 2)
        old = lax.rem(k + 1, 2)
        d_args = (drecv, ds_sem, dr_sem, par, me_r, "row", row_peers)
        p_args = (precv, ps_sem, pr_sem, par, me_c, "col", col_peers)
        flag_now = jnp.where(k <= ITERS - 3, restart_ref[k], 0) == 1

        if not first:
            tile(dyr, ys_sem, yr_sem, par, me_r, "row", row_peers, "start")
        y_low = y_s[...].astype(bf16)
        pieces = jnp.dot(oh_r[...], y_low, preferred_element_type=f32)
        products(pieces, k_v, drecv, me_r, par, d_args, first)
        if first:
            settle()
        else:
            both(precv, ps_sem, pr_sem, old, me_c, "col", col_peers, "sent")
            flag_old = jnp.where(k <= ITERS - 2, restart_ref[k - 1], 0) == 1
            tile(dyr, ys_sem, yr_sem, par, me_r, "row", row_peers, "wait")
            drift_x = total(dxr, old, n_col) / total_cols + epsilon
            drift_y = total(dyr, par, n_row) / total_rows + epsilon
            omega_next = jnp.sqrt(omega) * jnp.sqrt(jnp.sqrt(drift_x / drift_y))
            omega = jnp.where(flag_old, omega_next, omega)
        tau = step_scale / omega
        sigma = step_scale * omega

        dual = gather_sum(oh_d, d_args, n_row)
        x = x_s[...]
        x_next = jnp.minimum(jnp.maximum(x - tau * (obj_s[...] - dual), 0.0), ub_s[...])
        extrap = (2.0 * x_next - x).astype(bf16)
        pieces = jnp.dot(oh_c[...], extrap, preferred_element_type=f32)
        x_s[...] = x_next
        products(pieces, kt_v, precv, me_c, par, p_args, False)

        x_next = x_s[...]
        taken = taken + 1.0
        inv = 1.0 / taken
        sum_x = sx_s[...] + x_next
        mean_x = sum_x * inv
        gap = mean_x - ax_s[...]
        dxr[par, me_c] = fold(gap * gap)
        tile(dxr, xs_sem, xr_sem, par, me_c, "col", col_peers, "start")
        x_last = jnp.where(flag_now, mean_x, x_next)
        x_s[...] = x_last
        ax_s[...] = jnp.where(flag_now, mean_x, ax_s[...])
        sx_s[...] = jnp.where(flag_now, 0.0, sum_x)
        both(*d_args, "sent")
        if not first:

            @pl.when(k == ITERS - 1)
            def _():
                narrow(raw_x, x_s[...], col_blocks)
                out_x.start()

        primal = gather_sum(oh_p, p_args, n_col)
        y_next = jnp.maximum(y_s[...] + sigma * (dem_s[...] - primal), 0.0)
        sum_y = sy_s[...] + y_next
        mean_y = sum_y * inv
        gap = mean_y - ay_s[...]
        dyr[old, me_r] = fold(gap * gap)
        y_s[...] = jnp.where(flag_now, mean_y, y_next)
        ay_s[...] = jnp.where(flag_now, mean_y, ay_s[...])
        sy_s[...] = jnp.where(flag_now, 0.0, sum_y)
        taken = jnp.where(flag_now, 0.0, taken)
        tile(dxr, xs_sem, xr_sem, par, me_c, "col", col_peers, "wait")
        return omega, taken

    carry = body(0, (jnp.ones((1, 1), f32), jnp.zeros((1, 1), f32)), True)
    lax.fori_loop(1, ITERS, body, carry)
    narrow(raw_y, y_s[...], row_blocks)
    out_y.start()
    both(precv, ps_sem, pr_sem, (ITERS - 1) % 2, me_c, "col", col_peers, "sent")
    out_x.wait()
    out_y.wait()


def shards(
    block_values,
    block_rows,
    block_cols,
    live_count,
    objective,
    upper_bound,
    demand,
    primal_start,
    dual_start,
    restart_at,
):
    slots, block = block_values.shape[2], block_values.shape[3]
    n_row = lax.axis_size("row")
    n_col = lax.axis_size("col")
    row_blocks = demand.shape[0] // block
    col_blocks = objective.shape[0] // block
    wide = lambda v: v.reshape(-1, 128)
    f32, bf16 = jnp.float32, jnp.bfloat16
    vmem = pl.BlockSpec(memory_space=pltpu.VMEM)
    smem = pl.BlockSpec(memory_space=pltpu.SMEM)
    hbm = pl.BlockSpec(memory_space=pl.ANY)
    dma = pltpu.SemaphoreType.DMA
    x_shape, y_shape = (col_blocks, block), (row_blocks, block)
    x_out, y_out = pl.pallas_call(
        functools.partial(kernel, n_row, n_col, slots, block),
        out_shape=(
            jax.ShapeDtypeStruct((col_blocks * block // 128, 128), f32),
            jax.ShapeDtypeStruct((row_blocks * block // 128, 128), f32),
        ),
        in_specs=[
            hbm,
            vmem,
            vmem,
            smem,
            smem,
            hbm,
            hbm,
            hbm,
            hbm,
            hbm,
        ],
        out_specs=(hbm, hbm),
        scratch_shapes=[
            pltpu.VMEM((slots * block, block), bf16),
            pltpu.VMEM((slots * block, block), bf16),
            pltpu.VMEM((8, 128), jnp.int32),
            pltpu.VMEM((n_row, 8, 128), jnp.int32),
            pltpu.VMEM((n_col, 8, 128), jnp.int32),
            pltpu.VMEM((2, col_blocks, n_row * slots // 2), bf16),
            pltpu.VMEM((2, row_blocks, n_col * slots // 2), bf16),
            pltpu.VMEM((slots, col_blocks), bf16),
            pltpu.VMEM((slots, row_blocks), bf16),
            pltpu.VMEM((2, 2, n_row, slots // 2, block), bf16),
            pltpu.VMEM((2, 2, n_col, slots // 2, block), bf16),
            pltpu.VMEM((2, n_row, 1, 128), f32),
            pltpu.VMEM((2, n_col, 1, 128), f32),
            pltpu.VMEM((3, col_blocks * block // 128, 128), f32),
            pltpu.VMEM((2, row_blocks * block // 128, 128), f32),
            pltpu.VMEM(x_shape, f32),
            pltpu.VMEM(x_shape, f32),
            pltpu.VMEM(y_shape, f32),
            pltpu.VMEM(x_shape, f32),
            pltpu.VMEM(y_shape, f32),
            pltpu.VMEM(x_shape, f32),
            pltpu.VMEM(y_shape, f32),
            pltpu.VMEM(x_shape, f32),
            pltpu.VMEM(y_shape, f32),
            dma((slots // GROUP,)),
            dma((5,)),
            dma((2,)),
            dma((n_row,)),
            dma((n_row,)),
            dma((n_col,)),
            dma((n_col,)),
            dma((2, n_row, 2)),
            dma((2, n_row, 2)),
            dma((2, n_col, 2)),
            dma((2, n_col, 2)),
            dma((2, n_row)),
            dma((2, n_row)),
            dma((2, n_col)),
            dma((2, n_col)),
        ],
        compiler_params=pltpu.CompilerParams(collective_id=0, has_side_effects=True),
    )(
        block_values.reshape(slots * block, block),
        block_cols[0],
        block_rows[0],
        live_count,
        restart_at,
        wide(objective),
        wide(upper_bound),
        wide(demand),
        wide(primal_start),
        wide(dual_start),
    )
    return x_out.reshape(-1), y_out.reshape(-1)


def solution(mesh):
    placed = (
        P("row", "col", None, None, None),
        P("row", "col", None),
        P("row", "col", None),
        P("row", "col"),
        P("col"),
        P("col"),
        P("row"),
        P("col"),
        P("row"),
        P(),
    )
    return jax.shard_map(
        shards, mesh=mesh, in_specs=placed, out_specs=(P("col"), P("row")), check_vma=False
    )
```
